32 devices in a mesh: dp: 2 (over y), context: 2 (over x), expert: 8 (over z, core).
Axes of the slice: x: 2, y: 2, z: 4, core: 2. Of those that a mesh axis runs over, the one named last changes fastest.
Arguments:
- tokens: bfloat16 [2, 2048, 2048], P('dp', ('context', 'expert')), may hold values from -6 to 6
- cotangent: bfloat16 [2, 2048, 2048], P('dp', ('context', 'expert')), may hold values from -6 to 6
- routes: int32 [2, 2048, 8], P('dp', ('context', 'expert')), may hold values from 0 to 15, all different within a row; in each aligned block of 128 rows (0 to 127, 128 to 255, ..., all dimensions but the last counted through in order) at most 96 rows name the same one
- gain_attn: float32 [2048], replicated, may hold values from 0.5 to 1.5
- projection_weight: bfloat16 [2048, 5120], P(('dp', 'expert')), may hold values from -0.125 to 0.125
- q_gain: float32 [128], replicated, may hold values from 0.5 to 1.5
- k_gain: float32 [128], replicated, may hold values from 0.5 to 1.5
- w_out: bfloat16 [4096, 2048], P(('dp', 'expert')), may hold values from -1.5 to 1.5
- gain_ffn: float32 [2048], replicated, may hold values from 0.5 to 1.5
- w_router: float32 [2048, 16], replicated, may hold values from -0.25 to 0.25
- w_gate: bfloat16 [16, 2048, 768], P(('dp', 'expert')), may hold values from -0.125 to 0.125
- w_up: bfloat16 [16, 2048, 768], P(('dp', 'expert')), may hold values from -0.125 to 0.125
- w_down: bfloat16 [16, 768, 2048], P(('dp', 'expert')), may hold values from -0.625 to 0.625
Outputs:
- out_tokens: bfloat16 [2, 2048, 2048], P('dp', ('context', 'expert'))
- d_tokens: bfloat16 [2, 2048, 2048], P('dp', ('context', 'expert'))
- d_gain_attn: float32 [2048], replicated
- d_w_qkv: float32 [2048, 5120], P(('dp', 'expert'))
- d_q_gain: float32 [128], replicated
- d_k_gain: float32 [128], replicated
- d_w_out: float32 [4096, 2048], P(('dp', 'expert'))
- d_gain_ffn: float32 [2048], replicated
- d_w_router: float32 [2048, 16], replicated
- d_w_gate: float32 [16, 2048, 768], P(('dp', 'expert'))
- d_w_up: float32 [16, 2048, 768], P(('dp', 'expert'))
- d_w_down: float32 [16, 768, 2048], P(('dp', 'expert'))
The draws below stay inside these ranges and needn't reach their ends.
Inputs may be any that keep to these rules, and one draw needn't show every extreme that they name: `routes`: A row names 8 different experts. In each aligned block of 128 rows (the rows of one device) no expert is named by more than 96 rows, a bound that some block reaches.
All inputs are finite; a program needn't handle non-finite values.
Results may differ from the reference program's by a relative error of at most 0.022.
Values may be sent and summed in bfloat16 or wider, within the bound.
No kernel may reach another device: no remote copies, remote signals or barrier semaphores. Data moves between devices by JAX's collectives and lax.ppermute only.
A program may use at most 320 MiB of HBM per device.

```python
import math
import jax
import jax.numpy as jnp
import numpy as np
from jax import lax

MODEL_DIM = 2048
QUERY_HEADS = 32
KEY_VALUE_HEADS = 4
HEAD_DIM = 128
FF = 768
TOP = 8
TOK_DEV = 128
SEQUENCE_LENGTH = 2048
SEQUENCE_COUNT = 2
EXPERTS = 16
CAP = 96


def shard_levels(stream_key, shape, shards, least, top_value):
    gain = 1.0
    for dim, parts in shards:
        heights = jax.random.uniform(jax.random.fold_in(jax.random.fold_in(stream_key, 6), dim), (parts,), jnp.float32, least / len(shards), top_value / len(shards))
        gain = gain * jnp.repeat(jnp.exp(heights), shape[dim] // parts).reshape((-1,) + (1,) * (len(shape) - 1 - dim))
    return gain


def routed_block(rng, own, number, rows, count, top, bound, skew):
    order = jax.random.permutation(rng, count)
    crowded, ordinary = load_shares(count, rows * top, bound, skew, True), load_shares(count, rows * top, bound, skew, False)
    places = jnp.arange(count)

    def named(sizes, offset_by):
        used = int((sizes > 0).sum())
        fixed = max(1, used // 4)
        moved = fixed + (places - fixed + offset_by * (used - fixed)) % max(1, count - fixed)
        return jnp.zeros((count,), jnp.int32).at[order[jnp.where(places < fixed, places, moved)]].set(jnp.asarray(sizes, jnp.int32))

    sizes = jnp.where(number % 4 == 0, named(crowded, number // 4), named(ordinary, number - number // 4 - 1))
    mixed = jax.random.permutation(jax.random.fold_in(own, 3), count)
    donor, receiver = mixed[0:count // 2 * 2:2], mixed[1:count // 2 * 2:2]
    room = jnp.minimum(sizes[donor] - 1, bound - sizes[receiver]) // 2
    room = jnp.where((donor == order[0]) | (receiver == order[0]) | (sizes[receiver] == 0), 0, jnp.maximum(room, 0))
    moved = jax.random.randint(jax.random.fold_in(own, 4), (count // 2,), 0, 1 << 20) % (room + 1)
    sizes = sizes.at[donor].add(-moved).at[receiver].add(moved)
    labels = jnp.searchsorted(jnp.cumsum(sizes), jnp.arange(rows * top), side="right").astype(jnp.int32)
    table = labels.reshape(top, rows).T
    table = table[jax.random.permutation(jax.random.fold_in(own, 1), rows)]
    offset_by = jax.random.randint(jax.random.fold_in(own, 2), (rows, 1), 0, top)
    return jnp.take_along_axis(table, (jnp.arange(top)[None, :] + offset_by) % top, axis=1)


def load_shares(number_of, total, reach, lean, full):
    weights = [(1 << 20) // math.isqrt(rank ** lean) + 1 for rank in range(1, number_of + 1)]
    largest = reach if full else min(reach, max(-(-total // number_of), total * weights[0] // sum(weights)))
    least = 1 if total - largest >= number_of - 1 else 0
    counts, spare = [largest] + [least] * (number_of - 1), total - largest - least * (number_of - 1)
    while spare > 0:
        movable = [i for i in range(1, number_of) if counts[i] < largest] or [i for i in range(1, number_of) if counts[i] < reach]
        mass, left = sum([weights[i] for i in movable]), spare
        for i in movable:
            more = min(reach - counts[i], max(1, left * weights[i] // mass), spare)
            counts[i] = counts[i] + more
            spare = spare - more
    return np.array(counts)


def noise(rng, shape, width, bound, pieces=(), kind=jnp.bfloat16):
    factor_of = shard_levels(rng, shape, pieces, -0.22, 0.18) if pieces else 1.0
    array = jax.random.normal(rng, shape, jnp.float32) * width * factor_of
    return jnp.minimum(jnp.maximum(array, -bound), bound).astype(kind)


def setup_inputs(seed: int = 0) -> dict:
    splits = jax.random.split(jax.random.key(seed), 14)
    tokens = noise(splits[0], (SEQUENCE_COUNT, SEQUENCE_LENGTH, MODEL_DIM), 1.0, 6.0, ((0, 2), (1, 16)))
    cotangent = noise(splits[1], (SEQUENCE_COUNT, SEQUENCE_LENGTH, MODEL_DIM), 1.0, 6.0, ((0, 2), (1, 16)))
    routes_keys = jax.random.split(jax.random.fold_in(splits[2], 1), SEQUENCE_COUNT * SEQUENCE_LENGTH // TOK_DEV)
    routes_turns = jax.random.permutation(jax.random.fold_in(splits[2], 3), SEQUENCE_COUNT * SEQUENCE_LENGTH // TOK_DEV)
    routes = jax.vmap(lambda own, number: routed_block(jax.random.fold_in(splits[2], 2), own, number, TOK_DEV, EXPERTS, TOP, CAP, 2))(routes_keys, routes_turns).reshape((SEQUENCE_COUNT, SEQUENCE_LENGTH, TOP))
    gain_attn = jnp.clip(1.0 + 0.1 * jax.random.normal(splits[3], (MODEL_DIM,), jnp.float32), 0.5, 1.5)
    projection_weight = noise(splits[4], (MODEL_DIM, (QUERY_HEADS + 2 * KEY_VALUE_HEADS) * HEAD_DIM), MODEL_DIM ** -0.5, 0.125, ((0, 16),))
    q_gain = jnp.clip(1.0 + 0.1 * jax.random.normal(splits[5], (HEAD_DIM,), jnp.float32), 0.5, 1.5)
    k_gain = jnp.clip(1.0 + 0.1 * jax.random.normal(splits[6], (HEAD_DIM,), jnp.float32), 0.5, 1.5)
    w_out = noise(splits[7], (QUERY_HEADS * HEAD_DIM, MODEL_DIM), 16 ** -0.5, 1.5, ((0, 16),))
    gain_ffn = jnp.clip(1.0 + 0.1 * jax.random.normal(splits[8], (MODEL_DIM,), jnp.float32), 0.5, 1.5)
    w_router = noise(splits[9], (MODEL_DIM, EXPERTS), (MODEL_DIM // 4) ** -0.5, 0.25, (), jnp.float32)
    w_gate = noise(splits[10], (EXPERTS, MODEL_DIM, FF), MODEL_DIM ** -0.5, 0.125, ((0, 16),))
    w_up = noise(splits[11], (EXPERTS, MODEL_DIM, FF), MODEL_DIM ** -0.5, 0.125, ((0, 16),))
    w_down = noise(splits[12], (EXPERTS, FF, MODEL_DIM), (FF // 8) ** -0.5, 0.625, ((0, 16),))
    return dict(tokens=tokens, cotangent=cotangent, routes=routes, gain_attn=gain_attn, projection_weight=projection_weight, q_gain=q_gain, k_gain=k_gain, w_out=w_out, gain_ffn=gain_ffn, w_router=w_router, w_gate=w_gate, w_up=w_up, w_down=w_down)


EPS = 1e-06
THETA = 1000000.0

def rms_scale(values_in, gain_vector):
    return values_in * lax.rsqrt(lax.optimization_barrier(jnp.mean(values_in * values_in, axis=-1, keepdims=True)) + EPS) * gain_vector

def rope_tables(positions, feature):
    half_width = feature // 2
    frequency = THETA ** (-2.0 * jnp.arange(half_width, dtype=jnp.float32) / feature)
    angles = positions.astype(jnp.float32)[:, None] * frequency[None, :]
    return (jnp.cos(angles), jnp.sin(angles))

def head_prep(raw_heads, gain_vector, cosine, sine):
    normed = rms_scale(raw_heads, gain_vector)
    half_width = normed.shape[-1] // 2
    first_half = normed[..., :half_width]
    second_half = normed[..., half_width:]
    cos_rows = cosine[:, None, :]
    sin_rows = sine[:, None, :]
    return jnp.concatenate([first_half * cos_rows - second_half * sin_rows, second_half * cos_rows + first_half * sin_rows], axis=-1)

def swiglu(gate_part, up_part):
    return jax.nn.silu(gate_part) * up_part

def route_weights(normed, router, route_ids):
    logits = jnp.dot(normed, router, precision=lax.Precision.HIGHEST)
    picks = route_ids[:, :, None] == jnp.arange(router.shape[1], dtype=jnp.int32)[None, None, :]
    chosen = lax.optimization_barrier(jnp.sum(jnp.where(picks, logits[:, None, :], 0.0), axis=-1))
    raised = jnp.exp(chosen)
    return raised / lax.optimization_barrier(jnp.sum(raised, axis=-1, keepdims=True))

def grouping_rows(block, kv_count):
    length, head_count, feature = block.shape
    group_width = head_count // kv_count
    return block.reshape(length, kv_count, group_width, feature).transpose(1, 2, 0, 3).reshape(kv_count, group_width * length, feature)

def ungroup_rows(grouped, length):
    kv_count, count_rows, feature = grouped.shape
    group_width = count_rows // length
    return grouped.reshape(kv_count, group_width, length, feature).transpose(2, 0, 1, 3).reshape(length, kv_count * group_width, feature)

def ahead_rows(query_matrix, query_offsets, key_cols, value_cols):
    block_len = math.gcd(key_cols.shape[1], 1024)
    scaling = query_matrix.shape[2] ** (-0.5)
    queries = query_matrix.astype(jnp.float32)
    steps_needed = jnp.max(query_offsets) // block_len + 1

    def advance(step_index, state):
        running_output, exponent_sums = state
        begin_at = step_index * block_len
        key_block = lax.dynamic_slice_in_dim(key_cols, begin_at, block_len, 1).astype(jnp.float32)
        value_block = lax.dynamic_slice_in_dim(value_cols, begin_at, block_len, 1).astype(jnp.float32)
        scores = jnp.einsum('hqd,hkd->hqk', queries, key_block) * scaling
        key_pos = begin_at + jnp.arange(block_len, dtype=jnp.int32)
        allowed = key_pos[None, None, :] <= query_offsets[None, :, None]
        raised = jnp.where(allowed, jnp.exp(scores), 0.0)
        rounded = lax.optimization_barrier(raised.astype(jnp.bfloat16)).astype(jnp.float32)
        running_output = running_output + jnp.einsum('hqk,hkd->hqd', rounded, value_block)
        return (running_output, exponent_sums + lax.optimization_barrier(jnp.sum(raised, axis=-1)))
    start_state = (jnp.zeros(query_matrix.shape, jnp.float32), jnp.zeros(query_matrix.shape[:2], jnp.float32))
    return lax.fori_loop(0, steps_needed, advance, start_state)

def reverse_rows(query_matrix, query_offsets, grad_rows, log_totals, delta_terms, key_cols, value_cols, key_start, value_start):
    block_len = math.gcd(key_cols.shape[1], 1024)
    scaling = query_matrix.shape[2] ** (-0.5)
    queries = query_matrix.astype(jnp.float32)
    grad_out = grad_rows.astype(jnp.float32)
    steps_needed = jnp.max(query_offsets) // block_len + 1

    def advance(step_index, state):
        query_gradient, key_complete, value_complete = state
        begin_at = step_index * block_len
        key_block = lax.dynamic_slice_in_dim(key_cols, begin_at, block_len, 1).astype(jnp.float32)
        value_block = lax.dynamic_slice_in_dim(value_cols, begin_at, block_len, 1).astype(jnp.float32)
        scores = jnp.einsum('hqd,hkd->hqk', queries, key_block) * scaling
        key_pos = begin_at + jnp.arange(block_len, dtype=jnp.int32)
        allowed = key_pos[None, None, :] <= query_offsets[None, :, None]
        probability = jnp.where(allowed, jnp.exp(scores - log_totals[:, :, None]), 0.0)
        dprobs = jnp.einsum('hqd,hkd->hqk', grad_out, value_block)
        dscores = probability * (dprobs - delta_terms[:, :, None])
        dscore_round = lax.optimization_barrier(dscores.astype(jnp.bfloat16)).astype(jnp.float32)
        prob_round = lax.optimization_barrier(probability.astype(jnp.bfloat16)).astype(jnp.float32)
        query_gradient = query_gradient + jnp.einsum('hqk,hkd->hqd', dscore_round, key_block)
        key_part = jnp.einsum('hqk,hqd->hkd', dscore_round, queries) * scaling
        value_part = jnp.einsum('hqk,hqd->hkd', prob_round, grad_out)
        key_complete = lax.dynamic_update_slice_in_dim(key_complete, lax.dynamic_slice_in_dim(key_complete, begin_at, block_len, 1) + key_part, begin_at, 1)
        value_complete = lax.dynamic_update_slice_in_dim(value_complete, lax.dynamic_slice_in_dim(value_complete, begin_at, block_len, 1) + value_part, begin_at, 1)
        return (query_gradient, key_complete, value_complete)
    start_state = (jnp.zeros(query_matrix.shape, jnp.float32), key_start, value_start)
    query_gradient, key_complete, value_complete = lax.fori_loop(0, steps_needed, advance, start_state)
    return (query_gradient * scaling, key_complete, value_complete)

def reference(tokens, cotangent, routes, gain_attn, projection_weight, q_gain, k_gain, w_out, gain_ffn, w_router, w_gate, w_up, w_down):
    count_tokens = SEQUENCE_COUNT * SEQUENCE_LENGTH
    group_width = QUERY_HEADS // KEY_VALUE_HEADS
    x_in = tokens.reshape(count_tokens, MODEL_DIM).astype(jnp.float32)
    cot_in = cotangent.reshape(count_tokens, MODEL_DIM).astype(jnp.float32)
    route_ids = routes.reshape(count_tokens, TOP)
    positions = jnp.tile(jnp.arange(SEQUENCE_LENGTH, dtype=jnp.int32), SEQUENCE_COUNT)
    cosine, sine = rope_tables(positions, HEAD_DIM)
    normed_one = rms_scale(x_in, gain_attn).astype(jnp.bfloat16)
    projected_complete = jnp.dot(normed_one, projection_weight, preferred_element_type=jnp.float32)
    q_raw = projected_complete[:, :QUERY_HEADS * HEAD_DIM].reshape(count_tokens, QUERY_HEADS, HEAD_DIM)
    key_unrotated = projected_complete[:, QUERY_HEADS * HEAD_DIM:(QUERY_HEADS + KEY_VALUE_HEADS) * HEAD_DIM].reshape(count_tokens, KEY_VALUE_HEADS, HEAD_DIM)
    value_heads = projected_complete[:, (QUERY_HEADS + KEY_VALUE_HEADS) * HEAD_DIM:].astype(jnp.bfloat16).reshape(count_tokens, KEY_VALUE_HEADS, HEAD_DIM)
    query_rotated = head_prep(q_raw, q_gain, cosine, sine).astype(jnp.bfloat16)
    key_rotated = head_prep(key_unrotated, k_gain, cosine, sine).astype(jnp.bfloat16)
    q_block = math.gcd(SEQUENCE_LENGTH, 512)
    q_steps = SEQUENCE_LENGTH // q_block
    q_seq = query_rotated.reshape(SEQUENCE_COUNT, q_steps, q_block, QUERY_HEADS, HEAD_DIM)
    key_sequence = key_rotated.reshape(SEQUENCE_COUNT, SEQUENCE_LENGTH, KEY_VALUE_HEADS, HEAD_DIM).transpose(0, 2, 1, 3)
    value_sequence = value_heads.reshape(SEQUENCE_COUNT, SEQUENCE_LENGTH, KEY_VALUE_HEADS, HEAD_DIM).transpose(0, 2, 1, 3)
    step_ids = jnp.arange(q_steps, dtype=jnp.int32)

    def seq_forward(packed):
        q_here, key_local, value_local = packed

        def one_block(piece):
            step_index, query_portion = piece
            query_offsets = jnp.tile(step_index * q_block + jnp.arange(q_block, dtype=jnp.int32), group_width)
            running_output, exponent_sums = ahead_rows(grouping_rows(query_portion, KEY_VALUE_HEADS), query_offsets, key_local, value_local)
            return (running_output / exponent_sums[:, :, None], exponent_sums)
        return lax.map(one_block, (step_ids, q_here))
    o_grouped, totals_all = lax.map(seq_forward, (q_seq, key_sequence, value_sequence))
    o_tokens = jax.vmap(jax.vmap(lambda grouped: ungroup_rows(grouped, q_block)))(o_grouped).reshape(count_tokens, QUERY_HEADS * HEAD_DIM)
    o_round = o_tokens.astype(jnp.bfloat16)
    x_mid = x_in + jnp.dot(o_round, w_out, preferred_element_type=jnp.float32)
    normed_two = rms_scale(x_mid, gain_ffn)
    normed_two_b = normed_two.astype(jnp.bfloat16)
    weights = route_weights(normed_two, w_router, route_ids)
    blocks = count_tokens // TOK_DEV
    pair_count = TOK_DEV * TOP
    flat_routes = route_ids.reshape(blocks, pair_count)
    hits = (flat_routes[:, :, None] == jnp.arange(EXPERTS, dtype=jnp.int32)[None, None, :]).astype(jnp.int32)
    slot = lax.optimization_barrier(jnp.sum((jnp.cumsum(hits, axis=1) - 1) * hits, axis=-1))
    home = jnp.arange(blocks, dtype=jnp.int32)[:, None] * CAP + slot
    flat_pick = flat_routes.reshape(-1)
    flat_home = home.reshape(-1)
    pair_ids = jnp.arange(count_tokens * TOP, dtype=jnp.int32)
    weights_flat = weights.reshape(-1)
    slot_total = blocks * CAP

    def expert_step(carry, packed):
        out_acc, dp_acc, dh_acc = carry
        expert_id, gate_mat, up_mat, down_mat = packed
        target = jnp.where(flat_pick == expert_id, flat_home, slot_total)
        owner = jnp.zeros((slot_total,), jnp.int32).at[target].set(pair_ids // TOP, mode='drop')
        pair_of = jnp.zeros((slot_total,), jnp.int32).at[target].set(pair_ids, mode='drop')
        live = jnp.zeros((slot_total,), jnp.float32).at[target].set(1.0, mode='drop')
        rows_in = jnp.where(live[:, None] > 0, normed_two_b[owner], jnp.zeros((), jnp.bfloat16))
        gate_val = jnp.dot(rows_in, gate_mat, preferred_element_type=jnp.float32)
        up_val = jnp.dot(rows_in, up_mat, preferred_element_type=jnp.float32)
        hidden = swiglu(gate_val, up_val).astype(jnp.bfloat16)
        y_rows = jnp.dot(hidden, down_mat, preferred_element_type=jnp.float32).astype(jnp.bfloat16)
        y_float = y_rows.astype(jnp.float32)
        share = weights_flat[pair_of] * live
        out_acc = out_acc.at[owner].add(share[:, None] * y_float)
        cot_rows = cot_in[owner]
        dp_acc = dp_acc.at[pair_of].add(lax.optimization_barrier(jnp.sum(cot_rows * y_float, axis=1)) * live)
        dy_rows = (share[:, None] * cot_rows).astype(jnp.bfloat16)
        dhidden = jnp.dot(dy_rows, down_mat.T, preferred_element_type=jnp.float32)
        unused, pull_glu = jax.vjp(swiglu, gate_val, up_val)
        dgate, dup = pull_glu(dhidden)
        dgate_b = dgate.astype(jnp.bfloat16)
        dup_b = dup.astype(jnp.bfloat16)
        grad_down = jnp.dot(hidden.T, dy_rows, preferred_element_type=jnp.float32)
        grad_gate = jnp.dot(rows_in.T, dgate_b, preferred_element_type=jnp.float32)
        grad_up = jnp.dot(rows_in.T, dup_b, preferred_element_type=jnp.float32)
        back_rows = (jnp.dot(dgate_b, gate_mat.T, preferred_element_type=jnp.float32) + jnp.dot(dup_b, up_mat.T, preferred_element_type=jnp.float32)).astype(jnp.bfloat16)
        dh_acc = dh_acc.at[owner].add(back_rows.astype(jnp.float32) * live[:, None])
        return ((out_acc, dp_acc, dh_acc), (grad_gate, grad_up, grad_down))
    start_carry = (jnp.zeros((count_tokens, MODEL_DIM), jnp.float32), jnp.zeros((count_tokens * TOP,), jnp.float32), jnp.zeros((count_tokens, MODEL_DIM), jnp.float32))
    (out_acc, dp_acc, dh_acc), (d_w_gate, d_w_up, d_w_down) = lax.scan(expert_step, start_carry, (jnp.arange(EXPERTS, dtype=jnp.int32), w_gate, w_up, w_down))
    out_tokens = (x_mid + out_acc).astype(jnp.bfloat16).reshape(SEQUENCE_COUNT, SEQUENCE_LENGTH, MODEL_DIM)
    unused, pull_route = jax.vjp(lambda normed, router: route_weights(normed, router, route_ids), normed_two, w_router)
    dh_route, d_w_router = pull_route(dp_acc.reshape(count_tokens, TOP))
    dh_two = dh_acc + dh_route
    unused, pull_norm_two = jax.vjp(rms_scale, x_mid, gain_ffn)
    dx_norm_two, d_gain_ffn = pull_norm_two(dh_two)
    dx_mid = cot_in + dx_norm_two
    da_round = dx_mid.astype(jnp.bfloat16)
    d_w_out = jnp.dot(o_round.T, da_round, preferred_element_type=jnp.float32)
    output_grad_round = jnp.dot(da_round, w_out.T, preferred_element_type=jnp.float32).astype(jnp.bfloat16)
    do_seq = output_grad_round.reshape(SEQUENCE_COUNT, q_steps, q_block, QUERY_HEADS, HEAD_DIM)

    def seq_backward(packed):
        q_here, do_here, o_here, tot_here, key_local, value_local = packed

        def one_block(carry, piece):
            key_complete, value_complete = carry
            step_index, query_portion, output_grad_portion, o_rows, exponent_sums = piece
            query_offsets = jnp.tile(step_index * q_block + jnp.arange(q_block, dtype=jnp.int32), group_width)
            output_grad_rows = grouping_rows(output_grad_portion, KEY_VALUE_HEADS)
            delta_terms = lax.optimization_barrier(jnp.sum(output_grad_rows.astype(jnp.float32) * o_rows, axis=-1))
            query_gradient, key_complete, value_complete = reverse_rows(grouping_rows(query_portion, KEY_VALUE_HEADS), query_offsets, output_grad_rows, jnp.log(exponent_sums), delta_terms, key_local, value_local, key_complete, value_complete)
            return ((key_complete, value_complete), ungroup_rows(query_gradient, q_block))
        empty_columns = jnp.zeros((KEY_VALUE_HEADS, SEQUENCE_LENGTH, HEAD_DIM), jnp.float32)
        (key_complete, value_complete), query_grads = lax.scan(one_block, (empty_columns, empty_columns), (step_ids, q_here, do_here, o_here, tot_here))
        return (query_grads, key_complete, value_complete)
    dq_all, key_grad_total, value_grad_total = lax.map(seq_backward, (q_seq, do_seq, o_grouped, totals_all, key_sequence, value_sequence))
    dq_tok = dq_all.reshape(count_tokens, QUERY_HEADS, HEAD_DIM)
    key_grad_tokens = key_grad_total.transpose(0, 2, 1, 3).reshape(count_tokens, KEY_VALUE_HEADS, HEAD_DIM)
    value_grad_tokens = value_grad_total.transpose(0, 2, 1, 3).reshape(count_tokens, KEY_VALUE_HEADS * HEAD_DIM)
    unused, pull_query = jax.vjp(lambda raw, gains: head_prep(raw, gains, cosine, sine), q_raw, q_gain)
    query_grad_unrotated, d_q_gain = pull_query(dq_tok)
    unused, pull_key = jax.vjp(lambda raw, gains: head_prep(raw, gains, cosine, sine), key_unrotated, k_gain)
    key_grad_unrotated, d_k_gain = pull_key(key_grad_tokens)
    projection_grad = jnp.concatenate([query_grad_unrotated.reshape(count_tokens, QUERY_HEADS * HEAD_DIM), key_grad_unrotated.reshape(count_tokens, KEY_VALUE_HEADS * HEAD_DIM), value_grad_tokens], axis=1).astype(jnp.bfloat16)
    d_w_qkv = jnp.dot(normed_one.T, projection_grad, preferred_element_type=jnp.float32)
    dh_one = jnp.dot(projection_grad, projection_weight.T, preferred_element_type=jnp.float32)
    unused, pull_norm_one = jax.vjp(rms_scale, x_in, gain_attn)
    dx_norm_one, d_gain_attn = pull_norm_one(dh_one)
    d_tokens = (dx_mid + dx_norm_one).astype(jnp.bfloat16).reshape(SEQUENCE_COUNT, SEQUENCE_LENGTH, MODEL_DIM)
    return (out_tokens, d_tokens, d_gain_attn, d_w_qkv, d_q_gain, d_k_gain, d_w_out, d_gain_ffn, d_w_router, d_w_gate, d_w_up, d_w_down)
```

```python
import functools

import jax
import jax.numpy as jnp
from jax import lax
from jax.experimental import pallas as pl
from jax.experimental.pallas import tpu as pltpu
from jax.sharding import Mesh
from jax.sharding import PartitionSpec as P

QUERY_HEADS = 32
KEY_VALUE_HEADS = 4
HEAD_DIM = 128
TOP = 8
EPS = 1e-06
THETA = 1000000.0
SCALE = HEAD_DIM ** (-0.5)
VMEM_LIMIT = 60 * 1024 * 1024
ALL = ("dp", "context", "z", "core")
PLANE = ("dp", "z", "core")
GROUP = ("context", "core")
RING = ("dp", "z")
BF = jnp.bfloat16
F32 = jnp.float32


NT = (((1,), (1,)), ((), ()))


def rms_scale(values_in, gain_vector):
    return (
        values_in
        * lax.rsqrt(jnp.mean(values_in * values_in, axis=-1, keepdims=True) + EPS)
        * gain_vector
    )


def dot(a, b):
    return jnp.dot(a, b, preferred_element_type=F32)


def dot_nt(a, b):
    return lax.dot_general(a, b, NT, preferred_element_type=F32)


def dot_tn(a, b):
    return lax.dot_general(a, b, (((0,), (0,)), ((), ())), preferred_element_type=F32)


def row_sums(values):
    ones = jnp.ones((8, values.shape[1]), F32)
    return lax.dot_general(
        ones, values, NT, precision=lax.Precision.HIGHEST, preferred_element_type=F32
    )[0:1]


def rotate(x, gain, cos, sin):
    r = lax.rsqrt(jnp.mean(x * x, axis=-1, keepdims=True) + EPS)
    y = x * r * gain
    return y * cos + pltpu.roll(y, HEAD_DIM // 2, 1) * sin


def rotate_back(dy, x, gain, cos, sin):
    dn = dy * cos + pltpu.roll(dy * sin, HEAD_DIM // 2, 1)
    r = lax.rsqrt(jnp.mean(x * x, axis=-1, keepdims=True) + EPS)
    xh = x * r
    dgain = jnp.sum(dn * xh, axis=0, keepdims=True)
    dxn = dn * gain
    return r * (dxn - xh * jnp.mean(dxn * xh, axis=-1, keepdims=True)), dgain


def prep_q_kernel(x_ref, cos_ref, sin_ref, gain_ref, out_ref):
    out_ref[...] = rotate(x_ref[...], gain_ref[...], cos_ref[...], sin_ref[...]).astype(BF)


def prep_kv_kernel(k_ref, v_ref, cos_ref, sin_ref, gain_ref, out_ref):
    out_ref[:, :HEAD_DIM] = rotate(
        k_ref[...], gain_ref[...], cos_ref[...], sin_ref[...]
    ).astype(BF)
    out_ref[:, HEAD_DIM:] = v_ref[...].astype(BF)


def back_kv_kernel(d_ref, k_ref, cos_ref, sin_ref, gain_ref, out_ref, dgain_ref):
    dx, dgain = rotate_back(
        d_ref[:, :HEAD_DIM], k_ref[...], gain_ref[...], cos_ref[...], sin_ref[...]
    )
    out_ref[:, :HEAD_DIM] = dx.astype(BF)
    out_ref[:, HEAD_DIM:] = d_ref[:, HEAD_DIM:].astype(BF)
    dgain_ref[...] = dgain


def params(*semantics):
    return pltpu.CompilerParams(
        dimension_semantics=semantics, vmem_limit_bytes=VMEM_LIMIT
    )


def prep_q(qkv, cos, sin, gain, heads):
    rows = qkv.shape[0]
    full = pl.BlockSpec((rows, HEAD_DIM), lambda h: (0, 0))
    return pl.pallas_call(
        prep_q_kernel,
        grid=(heads,),
        in_specs=[
            pl.BlockSpec((rows, HEAD_DIM), lambda h: (0, h)),
            full,
            full,
            pl.BlockSpec((1, HEAD_DIM), lambda h: (0, 0)),
        ],
        out_specs=pl.BlockSpec((None, rows, HEAD_DIM), lambda h: (h, 0, 0)),
        out_shape=jax.ShapeDtypeStruct((heads, rows, HEAD_DIM), BF),
        compiler_params=params("arbitrary"),
        name="prep_q",
    )(qkv, cos, sin, gain)


def prep_kv(qkv, cos, sin, gain, heads):
    rows = qkv.shape[0]
    full = pl.BlockSpec((rows, HEAD_DIM), lambda i: (0, 0))
    return pl.pallas_call(
        prep_kv_kernel,
        grid=(1,),
        in_specs=[
            pl.BlockSpec((rows, HEAD_DIM), lambda i: (0, heads)),
            pl.BlockSpec((rows, HEAD_DIM), lambda i: (0, heads + 1)),
            full,
            full,
            pl.BlockSpec((1, HEAD_DIM), lambda i: (0, 0)),
        ],
        out_specs=pl.BlockSpec((rows, 2 * HEAD_DIM), lambda i: (0, 0)),
        out_shape=jax.ShapeDtypeStruct((rows, 2 * HEAD_DIM), BF),
        compiler_params=params("arbitrary"),
        name="prep_kv",
    )(qkv, qkv, cos, sin, gain)


def back_kv(dkv, qkv, cos, sin, gain, heads):
    rows = qkv.shape[0]
    full = pl.BlockSpec((rows, HEAD_DIM), lambda i: (0, 0))
    one = pl.BlockSpec((1, HEAD_DIM), lambda i: (0, 0))
    wide = pl.BlockSpec((rows, 2 * HEAD_DIM), lambda i: (0, 0))
    return pl.pallas_call(
        back_kv_kernel,
        grid=(1,),
        in_specs=[
            wide,
            pl.BlockSpec((rows, HEAD_DIM), lambda i: (0, heads)),
            full,
            full,
            one,
        ],
        out_specs=[wide, one],
        out_shape=[
            jax.ShapeDtypeStruct((rows, 2 * HEAD_DIM), BF),
            jax.ShapeDtypeStruct((1, HEAD_DIM), F32),
        ],
        compiler_params=params("arbitrary"),
        name="back_kv",
    )(dkv, qkv, cos, sin, gain)


def chunk_offset(m, ctx, depth, size):
    return pl.multiple_of((lax.rem(m, depth) * ctx + lax.div(m, depth)) * size, size)


def attn_forward_kernel(ctx, depth, z_ref, q_ref, kv_ref, o_ref, ob_ref, tot_ref, acc, lac):
    heads, size, feature = q_ref.shape
    last = pl.program_id(0) * depth + z_ref[0]
    acc[...] = jnp.zeros_like(acc)
    lac[...] = jnp.zeros_like(lac)

    def chunk(m, masked):
        off = chunk_offset(m, ctx, depth, size)
        keys = kv_ref[pl.ds(off, size), 0:feature]
        values = kv_ref[pl.ds(off, size), feature : 2 * feature]
        if masked:
            allowed = lax.broadcasted_iota(jnp.int32, (size, size), 1) <= lax.broadcasted_iota(
                jnp.int32, (size, size), 0
            )
        for h in range(heads):
            e = jnp.exp(dot_nt(q_ref[h], keys) * SCALE)
            if masked:
                e = jnp.where(allowed, e, 0.0)
            acc[h] += dot(e.astype(BF), values)
            part = e[:, 0:feature]
            for j in range(1, size // feature):
                part = part + e[:, j * feature : (j + 1) * feature]
            lac[h] += part

    def step(m, carry):
        chunk(m, False)
        return carry

    lax.fori_loop(0, last, step, 0)
    chunk(last, True)
    for h in range(heads):
        total = jnp.sum(lac[h], axis=-1, keepdims=True)
        o = acc[h] / total
        o_ref[:, h * feature : (h + 1) * feature] = o
        ob_ref[:, h * feature : (h + 1) * feature] = o.astype(BF)
        tot_ref[h : h + 1, :] = jnp.log(row_sums(lac[h]))


def attend_forward(q, kv, z, ctx, depth):
    heads, rows, feature = q.shape
    size = rows // ctx
    keys = kv.shape[0]
    width = heads * feature
    work = heads * size * size * feature * ctx * (ctx + 1) * depth // 2
    grid_spec = pltpu.PrefetchScalarGridSpec(
        num_scalar_prefetch=1,
        grid=(ctx,),
        in_specs=[
            pl.BlockSpec((heads, size, feature), lambda i, s: (0, i, 0)),
            pl.BlockSpec((keys, 2 * feature), lambda i, s: (0, 0)),
        ],
        out_specs=[
            pl.BlockSpec((size, width), lambda i, s: (i, 0)),
            pl.BlockSpec((size, width), lambda i, s: (i, 0)),
            pl.BlockSpec((heads, size), lambda i, s: (0, i)),
        ],
        scratch_shapes=[
            pltpu.VMEM((heads, size, feature), F32),
            pltpu.VMEM((heads, size, feature), F32),
        ],
    )
    return pl.pallas_call(
        functools.partial(attn_forward_kernel, ctx, depth),
        grid_spec=grid_spec,
        out_shape=[
            jax.ShapeDtypeStruct((rows, width), F32),
            jax.ShapeDtypeStruct((rows, width), BF),
            jax.ShapeDtypeStruct((heads, rows), F32),
        ],
        compiler_params=params("arbitrary"),
        cost_estimate=pl.CostEstimate(
            flops=4 * work, bytes_accessed=8 * rows * width, transcendentals=work // feature
        ),
        name="attn_forward",
    )(z, q, kv)


def attn_backward_kernel(
    ctx,
    depth,
    z_ref,
    q_ref,
    do_ref,
    o_ref,
    lse_ref,
    kv_ref,
    raw_ref,
    cos_ref,
    sin_ref,
    gain_ref,
    dq_ref,
    dgain_ref,
    dkv_ref,
    dqt,
    delta,
):
    heads, size, feature = q_ref.shape
    last = pl.program_id(0) * depth + z_ref[0]
    dqt[...] = jnp.zeros_like(dqt)

    @pl.when(pl.program_id(0) == 0)
    def _():
        dkv_ref[...] = jnp.zeros_like(dkv_ref)
        dgain_ref[...] = jnp.zeros_like(dgain_ref)

    for h in range(heads):
        cols = slice(h * feature, (h + 1) * feature)
        delta[h : h + 1, :] = row_sums(do_ref[:, cols].astype(F32) * o_ref[:, cols])

    def chunk(m, masked):
        off = chunk_offset(m, ctx, depth, size)
        keys = kv_ref[pl.ds(off, size), 0:feature]
        values = kv_ref[pl.ds(off, size), feature : 2 * feature]
        keys_t = keys.T
        if masked:
            allowed = lax.broadcasted_iota(jnp.int32, (size, size), 0) <= lax.broadcasted_iota(
                jnp.int32, (size, size), 1
            )
        dk = jnp.zeros((size, feature), F32)
        dv = jnp.zeros((size, feature), F32)
        for h in range(heads):
            q = q_ref[h]
            do = do_ref[:, h * feature : (h + 1) * feature]
            p = jnp.exp(dot_nt(keys, q) * SCALE - lse_ref[h : h + 1, :])
            if masked:
                p = jnp.where(allowed, p, 0.0)
            ds = (p * (dot_nt(values, do) - delta[h : h + 1, :])).astype(BF)
            dv += dot(p.astype(BF), do)
            dk += dot(ds, q)
            dqt[h] += dot(keys_t, ds)
        dkv_ref[pl.ds(off, size), 0:feature] += dk * SCALE
        dkv_ref[pl.ds(off, size), feature : 2 * feature] += dv

    def step(m, carry):
        chunk(m, False)
        return carry

    lax.fori_loop(0, last, step, 0)
    chunk(last, True)
    dgain = jnp.zeros((1, feature), F32)
    for h in range(heads):
        cols = slice(h * feature, (h + 1) * feature)
        dx, dg = rotate_back(
            dqt[h].T * SCALE, raw_ref[:, cols], gain_ref[...], cos_ref[...], sin_ref[...]
        )
        dq_ref[:, cols] = dx.astype(BF)
        dgain += dg
    dgain_ref[...] += dgain


def attend_backward(q, do, o, lse, kv, qkv, cos, sin, gain, z, ctx, depth):
    heads, rows, feature = q.shape
    size = rows // ctx
    keys = kv.shape[0]
    width = heads * feature
    work = heads * size * size * feature * ctx * (ctx + 1) * depth // 2
    row_block = pl.BlockSpec((size, width), lambda i, s: (i, 0))
    table = pl.BlockSpec((size, feature), lambda i, s: (i, 0))
    one = pl.BlockSpec((1, feature), lambda i, s: (0, 0))
    every = pl.BlockSpec((keys, 2 * feature), lambda i, s: (0, 0))
    grid_spec = pltpu.PrefetchScalarGridSpec(
        num_scalar_prefetch=1,
        grid=(ctx,),
        in_specs=[
            pl.BlockSpec((heads, size, feature), lambda i, s: (0, i, 0)),
            row_block,
            row_block,
            pl.BlockSpec((heads, size), lambda i, s: (0, i)),
            every,
            row_block,
            table,
            table,
            one,
        ],
        out_specs=[row_block, one, every],
        scratch_shapes=[
            pltpu.VMEM((heads, feature, size), F32),
            pltpu.VMEM((heads, size), F32),
        ],
    )
    return pl.pallas_call(
        functools.partial(attn_backward_kernel, ctx, depth),
        grid_spec=grid_spec,
        out_shape=[
            jax.ShapeDtypeStruct((rows, width), BF),
            jax.ShapeDtypeStruct((1, feature), F32),
            jax.ShapeDtypeStruct((keys, 2 * feature), F32),
        ],
        compiler_params=params("arbitrary"),
        cost_estimate=pl.CostEstimate(
            flops=10 * work, bytes_accessed=16 * rows * width, transcendentals=work // feature
        ),
        name="attn_backward",
    )(z, q, do, o, lse, kv, qkv, cos, sin, gain)


def moe_kernel(
    h_ref, c_ref, p_ref, wg_ref, wu_ref, wd_ref, hp_ref, dg_ref, du_ref, dx_ref, dp_ref
):
    h = h_ref[...]
    g = dot(h, wg_ref[...])
    u = dot(h, wu_ref[...])
    r = dot_nt(c_ref[...], wd_ref[...])
    p = p_ref[...]
    s = jax.nn.sigmoid(g)
    silu = g * s
    hid = silu * u
    hp_ref[...] = (p * hid).astype(BF)
    dp_ref[...] = row_sums(hid * r)
    dh = p * r
    dg = (dh * u * (s * (1.0 + g * (1.0 - s)))).astype(BF)
    du = (dh * silu).astype(BF)
    dg_ref[...] = dg
    du_ref[...] = du
    dx_ref[...] = (dot_nt(dg, wg_ref[...]) + dot_nt(du, wu_ref[...])).astype(BF)


def moe(h2, c, p, wg, wu, wd):
    rows, width = h2.shape
    ff = wg.shape[1]
    tile = min(rows, 256)
    wide = pl.BlockSpec((tile, width), lambda i: (i, 0))
    narrow = pl.BlockSpec((tile, ff), lambda i: (i, 0))

    def whole(a):
        return pl.BlockSpec(a.shape, lambda i: (0, 0), pipeline_mode=pl.Buffered(1))

    return pl.pallas_call(
        moe_kernel,
        grid=(rows // tile,),
        in_specs=[
            wide,
            wide,
            pl.BlockSpec((tile, 1), lambda i: (i, 0)),
            whole(wg),
            whole(wu),
            whole(wd),
        ],
        out_specs=[narrow, narrow, narrow, wide, pl.BlockSpec((1, tile), lambda i: (0, i))],
        out_shape=[
            jax.ShapeDtypeStruct((rows, ff), BF),
            jax.ShapeDtypeStruct((rows, ff), BF),
            jax.ShapeDtypeStruct((rows, ff), BF),
            jax.ShapeDtypeStruct((rows, width), BF),
            jax.ShapeDtypeStruct((1, rows), F32),
        ],
        compiler_params=params("arbitrary"),
        cost_estimate=pl.CostEstimate(
            flops=10 * rows * width * ff, bytes_accessed=8 * rows * width, transcendentals=rows * ff
        ),
        name="moe",
    )(h2, c, p, wg, wu, wd)


def swap(v, axis):
    return lax.ppermute(v, axis, [(0, 1), (1, 0)])


def butterfly(v, sizes):
    for axis in ("core", "context", "dp", "z"):
        count = sizes[axis]
        if count & (count - 1):
            v = lax.psum(v, axis)
            continue
        shift = 1
        while shift < count:
            v = v + lax.ppermute(v, axis, [(i, i ^ shift) for i in range(count)])
            shift *= 2
    return v


def pairs(sizes):
    return sizes["context"] == 2 and sizes["core"] == 2


def gather_group(v, c, k, sizes):
    if not pairs(sizes):
        return lax.all_gather(v, GROUP, axis=0, tiled=True)
    other = swap(v, "context")
    both = jnp.stack([jnp.where(c == 0, v, other), jnp.where(c == 0, other, v)])
    away = swap(both, "core")
    out = jnp.stack([jnp.where(k == 0, both, away), jnp.where(k == 0, away, both)], axis=1)
    return out.reshape((4 * v.shape[0],) + v.shape[1:])


def scatter_group(v, c, k, sizes):
    if not pairs(sizes):
        return lax.psum_scatter(v, GROUP, scatter_dimension=0, tiled=True).astype(F32)
    rows = v.shape[0] // 4
    parts = v.reshape(2, 2, rows, v.shape[1])
    mine = lax.dynamic_index_in_dim(parts, k, 1, keepdims=False)
    theirs = lax.dynamic_index_in_dim(parts, 1 - k, 1, keepdims=False)
    got = swap(theirs, "core")
    here = lax.dynamic_index_in_dim(mine, c, 0, keepdims=False).astype(
        F32
    ) + lax.dynamic_index_in_dim(got, c, 0, keepdims=False).astype(F32)
    there = lax.dynamic_index_in_dim(mine, 1 - c, 0, keepdims=False).astype(
        F32
    ) + lax.dynamic_index_in_dim(got, 1 - c, 0, keepdims=False).astype(F32)
    return here + swap(there.astype(BF), "context").astype(F32)


def local(
    sizes,
    tokens,
    cotangent,
    routes,
    gain_attn,
    projection_weight,
    q_gain,
    k_gain,
    w_out,
    gain_ffn,
    w_router,
    w_gate,
    w_up,
    w_down,
):
    dp, ctx, depth, cores = (sizes[a] for a in ALL)
    d_id, c_id, z_id, k_id = (lax.axis_index(a) for a in ALL)
    n, width = tokens.shape[1:]
    experts = w_router.shape[1]
    groups = ctx * cores
    heads = QUERY_HEADS // groups
    per_kv = QUERY_HEADS // KEY_VALUE_HEADS
    q_cols = heads * HEAD_DIM
    q_all = QUERY_HEADS * HEAD_DIM
    kv_all = KEY_VALUE_HEADS * HEAD_DIM
    rows_own = projection_weight.shape[0]
    tokens_group = groups * n
    expert_id = (d_id * depth + z_id) * cores + k_id

    def linear(d, c, z, k):
        return ((d * ctx + c) * depth + z) * cores + k

    x_in = tokens.reshape(n, width).astype(F32)
    cot_b = cotangent.reshape(n, width)
    cot_in = cot_b.astype(F32)
    route_ids = routes.reshape(n, TOP)

    q_part = lax.dynamic_slice_in_dim(projection_weight, c_id * cores * q_cols, cores * q_cols, 1)
    sends = []
    for k in range(cores):
        kv_head = ((c_id * cores + k) * heads) // per_kv
        sends.append(
            jnp.concatenate(
                [
                    q_part[:, k * q_cols : (k + 1) * q_cols],
                    lax.dynamic_slice_in_dim(
                        projection_weight, q_all + kv_head * HEAD_DIM, HEAD_DIM, 1
                    ),
                    lax.dynamic_slice_in_dim(
                        projection_weight, q_all + kv_all + kv_head * HEAD_DIM, HEAD_DIM, 1
                    ),
                ],
                axis=1,
            )
        )
    w_pair = lax.all_to_all(jnp.stack(sends), "core", split_axis=0, concat_axis=0, tiled=True)
    w_cols = lax.all_gather(
        w_pair.reshape(cores * rows_own, q_cols + 2 * HEAD_DIM), RING, axis=0, tiled=True
    )

    out_rows = w_out.shape[0]
    pieces = dp * depth
    piece = q_cols // pieces
    halves = out_rows // piece
    moves = []
    for i in range(halves):
        links = []
        for d in range(dp):
            for z in range(depth):
                for k in range(cores):
                    index = ((d * depth + z) * cores + k) * halves + i
                    group, j = divmod(index, pieces)
                    links.append(((d, group // cores, z, k), (j // depth, group // cores, j % depth, group % cores)))
        moves.append(links)
    w_piece = sum(
        lax.ppermute(
            w_out[i * piece : (i + 1) * piece],
            ALL,
            [(linear(*a), linear(*b)) for a, b in moves[i]],
        )
        for i in range(halves)
    )
    wo_rows = lax.all_gather(w_piece, RING, axis=0, tiled=True)

    normed_one = rms_scale(x_in, gain_attn).astype(BF)
    h1 = gather_group(normed_one, c_id, k_id, sizes)
    blocks = (
        jnp.arange(ctx, dtype=jnp.int32)[:, None] * (depth * cores)
        + z_id * cores
        + jnp.arange(cores, dtype=jnp.int32)[None, :]
    )
    positions = (
        blocks[:, :, None] * n + jnp.arange(n, dtype=jnp.int32)[None, None, :]
    ).reshape(tokens_group)
    half = HEAD_DIM // 2
    frequency = THETA ** (-2.0 * jnp.arange(half, dtype=F32) / HEAD_DIM)
    angles = positions.astype(F32)[:, None] * frequency[None, :]
    cosine, sine = jnp.cos(angles), jnp.sin(angles)
    cos = jnp.concatenate([cosine, cosine], axis=1)
    sin = jnp.concatenate([-sine, sine], axis=1)
    q_gain_row = q_gain.reshape(1, HEAD_DIM)
    k_gain_row = k_gain.reshape(1, HEAD_DIM)

    qkv = dot(h1, w_cols)
    kv_own = prep_kv(qkv, cos, sin, k_gain_row, heads)
    kv = lax.all_gather(kv_own, "z", axis=0, tiled=True)
    q = prep_q(qkv, cos, sin, q_gain_row, heads)
    z_arr = z_id.reshape(1).astype(jnp.int32)
    o, o_b, lse = attend_forward(q, kv, z_arr, ctx, depth)
    x_mid = x_in + scatter_group(dot(o_b, wo_rows).astype(BF), c_id, k_id, sizes)

    h2 = rms_scale(x_mid, gain_ffn)
    h2_b = h2.astype(BF)
    logits = jnp.dot(h2, w_router, precision=lax.Precision.HIGHEST)
    named = jnp.any(
        route_ids[:, :, None] == jnp.arange(experts, dtype=jnp.int32)[None, None, :], axis=1
    )
    raised = jnp.where(named, jnp.exp(logits), 0.0)
    p = raised / jnp.sum(raised, axis=-1, keepdims=True)

    h2_all = lax.all_gather(h2_b, PLANE, axis=0, tiled=True)
    c_all = lax.all_gather(cot_b, PLANE, axis=0, tiled=True)
    p_here = lax.all_to_all(p.T, PLANE, split_axis=0, concat_axis=0, tiled=True)
    hp, dg, du, dx, dprob = moe(
        h2_all, c_all, p_here.reshape(experts * n, 1), w_gate[0], w_up[0], w_down[0]
    )
    dh_experts = lax.psum_scatter(dx, PLANE, scatter_dimension=0, tiled=True).astype(F32)
    dp_own = lax.all_to_all(
        dprob.reshape(experts, n), PLANE, split_axis=0, concat_axis=0, tiled=True
    ).T
    y = dot(hp, w_down[0]).astype(BF)
    mixed = lax.psum_scatter(y, PLANE, scatter_dimension=0, tiled=True).astype(F32)
    out_tokens = (x_mid + mixed).astype(BF).reshape(tokens.shape)

    def both_contexts(v):
        v = v.astype(BF)
        if ctx == 2:
            return v.astype(F32) + swap(v, "context").astype(F32)
        return lax.psum(v, "context").astype(F32)

    grad_gate = both_contexts(dot_tn(h2_all, dg))
    grad_up = both_contexts(dot_tn(h2_all, du))
    grad_down = both_contexts(dot_tn(hp, c_all))

    dprob_own = jnp.where(named, dp_own, 0.0)
    dlogits = p * (dprob_own - jnp.sum(p * dprob_own, axis=-1, keepdims=True))
    grad_router_t = lax.dot_general(
        dlogits, h2, (((0,), (0,)), ((), ())), precision=lax.Precision.HIGHEST
    )
    dh2 = dh_experts + lax.dot_general(dlogits, w_router, NT, precision=lax.Precision.HIGHEST)
    unused, pull_norm_two = jax.vjp(rms_scale, x_mid, gain_ffn)
    dx_norm_two, grad_gain_ffn = pull_norm_two(dh2)
    dx_mid = cot_in + dx_norm_two
    da_own = dx_mid.astype(BF)
    early = butterfly(
        jnp.concatenate([grad_router_t, grad_gain_ffn[None]], axis=0), sizes
    )
    grad_router = early[:experts].T
    grad_gain_ffn = early[experts]

    da = gather_group(da_own, c_id, k_id, sizes)
    do = dot_nt(da, wo_rows).astype(BF)
    grad_out_part = lax.psum_scatter(
        dot_tn(o_b, da).astype(BF), RING, scatter_dimension=0, tiled=True
    )
    out_parts = []
    for i in range(halves):
        total = None
        for r in range(ctx):
            got = lax.ppermute(
                grad_out_part,
                ALL,
                [
                    (linear(*b), linear(a[0], (a[1] + r) % ctx, a[2], a[3]))
                    for a, b in moves[i]
                ],
            )
            total = got if total is None else total + got
        out_parts.append(total)
    grad_out = jnp.concatenate(out_parts, axis=0).astype(F32)

    dq_raw, grad_q_gain, dkv_all = attend_backward(
        q, do, o, lse, kv, qkv, cos, sin, q_gain_row, z_arr, ctx, depth
    )
    dkv = lax.psum_scatter(dkv_all.astype(BF), "z", scatter_dimension=0, tiled=True).astype(F32)
    dkv_raw, grad_k_gain = back_kv(dkv, qkv, cos, sin, k_gain_row, heads)
    dqkv = jnp.concatenate([dq_raw, dkv_raw], axis=1)
    dh1 = scatter_group(dot_nt(dqkv, w_cols).astype(BF), c_id, k_id, sizes)
    grad_cols = lax.psum_scatter(
        dot_tn(h1, dqkv).astype(BF), RING, scatter_dimension=0, tiled=True
    )
    grad_pair = lax.all_to_all(
        grad_cols.reshape(cores, rows_own, q_cols + 2 * HEAD_DIM),
        "core",
        split_axis=0,
        concat_axis=0,
        tiled=True,
    )
    grad_groups = lax.all_gather(grad_pair, "context", axis=0, tiled=True).astype(F32)

    def merged(v, count):
        v = v.reshape(count, groups // count, rows_own, v.shape[2]).sum(axis=1)
        return v.transpose(1, 0, 2).reshape(rows_own, count * v.shape[2])

    grad_qkv = jnp.concatenate(
        [
            merged(grad_groups[:, :, :q_cols], groups),
            merged(grad_groups[:, :, q_cols : q_cols + HEAD_DIM], KEY_VALUE_HEADS),
            merged(grad_groups[:, :, q_cols + HEAD_DIM :], KEY_VALUE_HEADS),
        ],
        axis=1,
    )
    unused, pull_norm_one = jax.vjp(rms_scale, x_in, gain_attn)
    dx_norm_one, grad_gain_attn = pull_norm_one(dh1)
    d_tokens = (dx_mid + dx_norm_one).astype(BF).reshape(tokens.shape)
    late = butterfly(
        jnp.concatenate([grad_gain_attn.reshape(-1, HEAD_DIM), grad_q_gain, grad_k_gain], axis=0),
        sizes,
    )
    return (
        out_tokens,
        d_tokens,
        late[:-2].reshape(width),
        grad_qkv,
        late[-2],
        late[-1],
        grad_out,
        grad_gain_ffn,
        grad_router,
        grad_gate[None],
        grad_up[None],
        grad_down[None],
    )


def solution(mesh):
    dp, ctx, expert = (mesh.shape[a] for a in ("dp", "context", "expert"))
    cores = 2 if expert % 2 == 0 else 1
    sizes = {"dp": dp, "context": ctx, "z": expert // cores, "core": cores}
    fine = Mesh(mesh.devices.reshape(tuple(sizes[a] for a in ALL)), ALL)
    token = P("dp", ("context", "z", "core"), None)
    matrix = P(PLANE, None)
    stack = P(PLANE, None, None)
    in_specs = (
        token,
        token,
        token,
        P(),
        matrix,
        P(),
        P(),
        matrix,
        P(),
        P(),
        stack,
        stack,
        stack,
    )
    out_specs = (
        token,
        token,
        P(),
        matrix,
        P(),
        P(),
        matrix,
        P(),
        P(),
        stack,
        stack,
        stack,
    )
    return jax.shard_map(
        functools.partial(local, sizes),
        mesh=fine,
        in_specs=in_specs,
        out_specs=out_specs,
        check_vma=False,
    )
```
